256 devices in a mesh: dp: 64 (over z, y, core), section: 4 (over x).
Axes of the slice: x: 4, y: 4, z: 8, core: 2. Of those that a mesh axis runs over, the one named last changes fastest.
Arguments:
- hidden_in: bfloat16 [4, 2, 64, 4096], P('section', None, 'dp'), may hold values from -48 to 48
- grad_out: bfloat16 [2, 64, 4096], P(None, 'dp'), may hold values from -6 to 6
- weight_gate: bfloat16 [4, 14336, 4096], P('section', 'dp'), may hold values from -0.09375 to 0.09375
- weight_up: bfloat16 [4, 14336, 4096], P('section', 'dp'), may hold values from -0.09375 to 0.09375
- weight_down: bfloat16 [4, 14336, 4096], P('section', 'dp'), may hold values from -0.046875 to 0.046875
- gain: float32 [4, 4096], P('section'), may hold values from 0.5 to 1.5
- counts: int32 [2], replicated, may hold values from 1 to 64, 85 in all
Outputs:
- grad_inputs: bfloat16 [4, 2, 64, 4096], P('section', None, 'dp')
- gate_grads: bfloat16 [4, 14336, 4096], P('section', 'dp')
- up_grads: bfloat16 [4, 14336, 4096], P('section', 'dp')
- down_grads: bfloat16 [4, 14336, 4096], P('section', 'dp')
- gain_grads: float32 [4, 4096], P('section')
The draws below stay inside these ranges and needn't reach their ends.
Inputs may be any that keep to these rules, and one draw needn't show every extreme that they name: The 2 counts sum to 85.
All inputs are finite; a program needn't handle non-finite values.
Results may differ from the reference program's by a relative error of at most 0.012.
Values may be sent and summed in bfloat16 or wider, within the bound.
No kernel may reach another device: no remote copies, remote signals or barrier semaphores. Data moves between devices by JAX's collectives and lax.ppermute only.
A program may use at most 128 MiB of HBM per device.

```python
import math
import jax
import jax.numpy as jnp
import numpy as np
from jax import lax

D = 4096
F = 14336
PMAX = 64
MB = 2
SECTIONS = 4


def draw_hidden_in(key, part):
    key_base = jax.random.fold_in(key, 11)
    key_column = jax.random.fold_in(key, 12)
    key_rowscale = jax.random.fold_in(key, 13)
    full_shape = (SECTIONS, MB, PMAX, D)
    column_scale = jnp.exp(jax.random.uniform(key_column, (SECTIONS, 1, 1, D), jnp.float32, 0.0, math.log(10.0)))
    row_scale = jnp.exp(jax.random.uniform(key_rowscale, (SECTIONS, MB, PMAX, 1), jnp.float32, math.log(0.1), 0.0))
    base_values = jax.random.truncated_normal(key_base, -4.0, 4.0, full_shape, jnp.float32)
    return (base_values * column_scale * row_scale).astype(jnp.bfloat16)


def level_of(key, dims, pieces, low, largest):
    level = 1.0
    for axis_at, blocks in pieces:
        draws = jax.random.uniform(jax.random.fold_in(jax.random.fold_in(key, 6), axis_at), (blocks,), jnp.float32, low / len(pieces), largest / len(pieces))
        level = level * jnp.repeat(jnp.exp(draws), dims[axis_at] // blocks).reshape((-1,) + (1,) * (len(dims) - 1 - axis_at))
    return level


def profile(number_of, total, most, skew):
    weights = [(1 << 20) // math.isqrt(grade ** skew) + 1 for grade in range(2, number_of + 1)]
    rest, given = total - most - (number_of - 1), [1] * (number_of - 1)
    while rest > 0:
        candidates = [i for i in range(number_of - 1) if given[i] < most]
        pool, left = sum([weights[i] for i in candidates]), rest
        for i in candidates:
            addition = min(most - given[i], max(1, left * weights[i] // pool), rest)
            given[i] = given[i] + addition
            rest = rest - addition
    return np.array([most] + given)


def uneven(stream_key, amount, total, limit, slope):
    if amount == 2:
        one = jax.random.randint(stream_key, (), max(1, total - limit), min(limit, total - 1) + 1)
        return jnp.stack([one, total - one])
    tallies = jnp.asarray(profile(amount, total, limit, slope), jnp.int32)
    twos = (amount - 1) // 2
    donor, receiver = tallies[1:1 + 2 * twos:2], tallies[2:2 + 2 * twos:2]
    room = jnp.minimum(donor - 1, limit - receiver)
    moved = jax.random.randint(jax.random.fold_in(stream_key, 1), (twos,), 0, 1 << 20) % (room + 1)
    tallies = tallies.at[1:1 + 2 * twos:2].set(donor - moved).at[2:2 + 2 * twos:2].set(receiver + moved)
    return tallies[jax.random.permutation(jax.random.fold_in(stream_key, 2), amount)]


def bell_draw(own_key, dims, spread, most, shards=(), held_as=jnp.bfloat16):
    entries = spread * jax.random.normal(own_key, dims, jnp.float32)
    if shards:
        entries = entries * level_of(own_key, dims, shards, -0.22, 0.18)
    return jnp.clip(entries, -most, most).astype(held_as)


def setup_inputs(seed: int = 0) -> dict:
    key_of = jax.random.split(jax.random.key(seed), 8)
    hidden_in = draw_hidden_in(jax.random.fold_in(key_of[7], 71), 0)
    grad_out = bell_draw(key_of[1], (MB, PMAX, D), 1.0, 6.0, ((1, 64),))
    weight_gate = bell_draw(key_of[2], (SECTIONS, F, D), D ** -0.5, 0.09375, ((0, 4), (1, 64)))
    weight_up = bell_draw(key_of[3], (SECTIONS, F, D), D ** -0.5, 0.09375, ((0, 4), (1, 64)))
    weight_down = bell_draw(key_of[4], (SECTIONS, F, D), F ** -0.5, 0.046875, ((0, 4), (1, 64)))
    gain = jnp.clip(1.0 + 0.1 * jax.random.normal(key_of[5], (SECTIONS, D), jnp.float32), 0.5, 1.5)
    counts = uneven(key_of[6], MB, 4 * PMAX // 3, PMAX, 2).astype(jnp.int32)
    return {"hidden_in": hidden_in, "grad_out": grad_out, "weight_gate": weight_gate, "weight_up": weight_up, "weight_down": weight_down, "gain": gain, "counts": counts}


def norm_rows(layer_rows, gain_row):
    row_values = layer_rows.astype(jnp.float32)
    inv_rms = lax.rsqrt(lax.optimization_barrier(jnp.mean(row_values * row_values, axis=-1, keepdims=True)) + 1e-05)
    normed_rows = (row_values * inv_rms * gain_row).astype(jnp.bfloat16)
    return (inv_rms, normed_rows)

def unit_grads(upstream, gate_pre, up_pre, down_mat):
    sigmoid_pre = jax.nn.sigmoid(gate_pre)
    silu_pre = gate_pre * sigmoid_pre
    activation = (silu_pre * up_pre).astype(jnp.bfloat16)
    grad_act = lax.dot_general(upstream, down_mat, (((1,), (1,)), ((), ())), preferred_element_type=jnp.float32)
    grad_gate = (grad_act * up_pre * sigmoid_pre * (1.0 + gate_pre * (1.0 - sigmoid_pre))).astype(jnp.bfloat16)
    grad_up = (grad_act * silu_pre).astype(jnp.bfloat16)
    return (activation, grad_gate, grad_up)

def norm_back(layer_rows, inv_rms, upstream, grad_normed, gain_row):
    row_values = layer_rows.astype(jnp.float32)
    gained_grad = gain_row * grad_normed
    inner_sum = lax.optimization_barrier(jnp.sum(gained_grad * row_values, axis=-1, keepdims=True))
    feature_count = row_values.shape[-1]
    grad_rows = upstream.astype(jnp.float32) + inv_rms * gained_grad - row_values * inv_rms ** 3 * inner_sum / feature_count
    return grad_rows.astype(jnp.bfloat16)

def contract_last(left_rows, right_rows):
    return lax.dot_general(left_rows, right_rows, (((1,), (1,)), ((), ())), preferred_element_type=jnp.float32)

def contract_first(left_rows, right_rows):
    return lax.dot_general(left_rows, right_rows, (((0,), (0,)), ((), ())), preferred_element_type=jnp.float32)

def reference(hidden_in, grad_out, weight_gate, weight_up, weight_down, gain, counts):
    slot_ids = jnp.arange(PMAX).astype(jnp.int32)
    live_slots = slot_ids[None, :] < counts[:, None]
    upstream = jnp.where(live_slots[:, :, None], grad_out, jnp.zeros((), jnp.bfloat16)).reshape(MB * PMAX, D)
    grad_list = []
    gate_list = []
    up_list = []
    down_list = []
    gain_list = []
    for section_pos in range(SECTIONS - 1, -1, -1):
        gate_mat = weight_gate[section_pos]
        up_mat = weight_up[section_pos]
        down_mat = weight_down[section_pos]
        gain_row = gain[section_pos]
        layer_rows = hidden_in[section_pos].reshape(MB * PMAX, D)
        inv_rms, normed_rows = norm_rows(layer_rows, gain_row)
        gate_pre = contract_last(normed_rows, gate_mat)
        up_pre = contract_last(normed_rows, up_mat)
        activation, grad_gate, grad_up = unit_grads(upstream, gate_pre, up_pre, down_mat)
        grad_normed = jnp.dot(grad_gate, gate_mat, preferred_element_type=jnp.float32)
        grad_normed = grad_normed + jnp.dot(grad_up, up_mat, preferred_element_type=jnp.float32)
        grad_rows = norm_back(layer_rows, inv_rms, upstream, grad_normed, gain_row)
        gain_part = lax.optimization_barrier(jnp.sum(grad_normed * layer_rows.astype(jnp.float32) * inv_rms, axis=0))
        gate_part = contract_first(grad_gate, normed_rows)
        up_part = contract_first(grad_up, normed_rows)
        down_part = contract_first(activation, upstream)
        upstream = grad_rows
        grad_list.append(grad_rows.reshape(MB, PMAX, D))
        gate_list.append(gate_part.astype(jnp.bfloat16))
        up_list.append(up_part.astype(jnp.bfloat16))
        down_list.append(down_part.astype(jnp.bfloat16))
        gain_list.append(gain_part)
    return (jnp.stack(grad_list[::-1]), jnp.stack(gate_list[::-1]), jnp.stack(up_list[::-1]), jnp.stack(down_list[::-1]), jnp.stack(gain_list[::-1]))
```

```python
import jax
import jax.numpy as jnp
from jax import lax
from jax.sharding import Mesh
from jax.sharding import PartitionSpec as P

NZ, NY, NC, NS = 8, 4, 2, 4
DP = ("z", "y", "core")
PLANE = ("z", "y")
LIVE = 85
GROUP = 24
USED = 22
ROWS = NY * GROUP
BF = jnp.bfloat16
F32 = jnp.float32


def dot_nt(a, b):
    return lax.dot_general(a, b, (((1,), (1,)), ((), ())), preferred_element_type=F32)


def dot_nn(a, b):
    return lax.dot_general(a, b, (((1,), (0,)), ((), ())), preferred_element_type=F32)


def dot_tn(a, b):
    return lax.dot_general(a, b, (((0,), (0,)), ((), ())), preferred_element_type=F32)


def row_of(micro, slot):
    position = jnp.where(micro == 0, slot, LIVE - 1 - slot)
    return GROUP * (position // USED) + position % USED


def swap_core(x):
    return lax.ppermute(x, "core", [(0, 1), (1, 0)])


def exchange(x):
    return lax.all_to_all(x, PLANE, 0, 0, tiled=True)


def gather_rows(hidden, top, counts, core):
    width = hidden.shape[-1]
    half = width // 2
    own = jnp.concatenate([hidden, top], axis=0).reshape(8, half)
    mine = exchange(jnp.broadcast_to(own[None], (NZ * NY, 8, half)))
    other = swap_core(mine)
    mine = mine.reshape(NZ * NY * 8, half)
    other = other.reshape(NZ * NY * 8, half)
    cols = lax.broadcasted_iota(jnp.int32, (ROWS, NZ * NY * 8), 1)
    rows = lax.broadcasted_iota(jnp.int32, (ROWS, NZ * NY * 8), 0)
    place, piece = cols // 8, cols % 8
    micro, part = (piece // 2) % 2, piece % 2
    limit = jnp.where(micro == 0, counts[0], counts[1])

    def pick(kind, of_core, at_half):
        slot = place * NC + of_core
        hit = (row_of(micro, slot) == rows) & (slot < limit) & (piece // 4 == kind) & (part == at_half)
        return hit.astype(BF)

    def build(kind):
        halves = []
        for at_half in range(2):
            total = dot_nn(pick(kind, core, at_half), mine) + dot_nn(pick(kind, 1 - core, at_half), other)
            halves.append(total.astype(BF))
        return jnp.concatenate(halves, axis=1)

    return build(0), build(1)


def on_device(hidden_in, grad_out, weight_gate, weight_up, weight_down, gain, counts):
    gate_mat, up_mat, down_mat = weight_gate[0], weight_up[0], weight_down[0]
    gain_row = gain[0]
    width = gate_mat.shape[1]
    half = width // 2
    lanes = width // (NC * NZ)
    z, y, core = lax.axis_index("z"), lax.axis_index("y"), lax.axis_index("core")
    section = lax.axis_index("section")

    hidden, upstream = gather_rows(hidden_in[0, :, 0], grad_out[:, 0], counts, core)
    values = hidden.astype(F32)
    inv_rms = lax.rsqrt(jnp.mean(values * values, axis=-1, keepdims=True) + 1e-05)
    normed = (values * inv_rms * gain_row).astype(BF)
    gate_pre = dot_nt(normed, gate_mat)
    up_pre = dot_nt(normed, up_mat)
    sig = jax.nn.sigmoid(gate_pre)
    silu = gate_pre * sig
    activation = (silu * up_pre).astype(BF)
    gate_factor = up_pre * sig * (1.0 + gate_pre * (1.0 - sig))

    def tile_of(x):
        rows = lax.dynamic_slice_in_dim(x, y * GROUP, GROUP, 0)
        return lax.dynamic_slice_in_dim(rows, core * half + z * lanes, lanes, 1)

    hidden_tile = tile_of(hidden).astype(F32)
    inv_tile = lax.dynamic_slice_in_dim(inv_rms, y * GROUP, GROUP, 0)
    gain_tile = lax.dynamic_slice_in_dim(gain_row, core * half + z * lanes, lanes, 0)
    in_group = lax.broadcasted_iota(jnp.int32, (NY, GROUP, 1), 1)
    tile_row = lax.broadcasted_iota(jnp.int32, (GROUP, 1), 0)

    for step in range(NS):
        last = step == NS - 1
        grad_act = dot_nt(upstream, down_mat)
        grad_gate = (grad_act * gate_factor).astype(BF)
        grad_up = (grad_act * silu).astype(BF)
        partial = dot_nn(grad_gate, gate_mat) + dot_nn(grad_up, up_mat)
        inner = jnp.sum(grad_gate.astype(F32) * gate_pre + grad_up.astype(F32) * up_pre, axis=1)
        inner = jnp.pad(inner.reshape(NY, GROUP), ((0, 0), (0, lanes - GROUP)))
        inner = jnp.tile(inner, (1, NC * NZ))
        packed = jnp.where(in_group == USED, inner[:, None, :], partial.reshape(NY, GROUP, width))
        if last:
            gain_part = jnp.sum(partial * (values * inv_rms), axis=0)
            packed = jnp.where(in_group == USED + 1, gain_part, packed)
        packed = packed.astype(BF).reshape(ROWS, width)
        away = lax.dynamic_slice_in_dim(packed, (1 - core) * half, half, 1)
        kept = lax.dynamic_slice_in_dim(packed, core * half, half, 1)
        summed = (kept.astype(F32) + swap_core(away).astype(F32)).astype(BF)
        pieces = summed.reshape(NY, GROUP, NZ, lanes).transpose(2, 0, 1, 3).reshape(NZ * NY, GROUP, lanes)
        total = jnp.sum(exchange(pieces).astype(F32), axis=0)
        up_tile = tile_of(upstream)
        row_sum = total[USED, :GROUP][:, None]
        grad_tile = (
            up_tile.astype(F32)
            + inv_tile * (gain_tile * total)
            - hidden_tile * inv_tile * inv_tile * row_sum / width
        )
        grad_tile = jnp.where(tile_row < USED, grad_tile, 0.0).astype(BF)
        if last:
            gain_sum = total[USED + 1]
            high = gain_sum.astype(BF)
            low = (gain_sum - high.astype(F32)).astype(BF)
            grad_tile = jnp.where(tile_row == USED, high, grad_tile)
            grad_tile = jnp.where(tile_row == USED + 1, low, grad_tile)
        else:
            moved = lax.ppermute(grad_tile, "section", [(NS - 1 - step, NS - 2 - step)])
            grad_tile = jnp.where(section == NS - 2 - step, moved, up_tile)
        spread = exchange(jnp.broadcast_to(grad_tile[None], (NZ * NY, GROUP, lanes)))
        mine = spread.reshape(NZ, NY, GROUP, lanes).transpose(1, 2, 0, 3).reshape(ROWS, half)
        other = swap_core(mine)
        gathered = jnp.concatenate(
            [jnp.where(core == 0, mine, other), jnp.where(core == 0, other, mine)], axis=1
        )
        if not last:
            upstream = gathered

    gate_grads = dot_tn(grad_gate, normed).astype(BF)
    up_grads = dot_tn(grad_up, normed).astype(BF)
    down_grads = dot_tn(activation, upstream).astype(BF)
    slot = z * NY * NC + y * NC + core
    micro = lax.broadcasted_iota(jnp.int32, (2, ROWS), 0)
    rows = lax.broadcasted_iota(jnp.int32, (2, ROWS), 1)
    limit = jnp.where(micro == 0, counts[0], counts[1])
    own_rows = ((row_of(micro, slot) == rows) & (slot < limit)).astype(BF)
    grad_rows = dot_nn(own_rows, gathered).astype(BF)
    gain_grads = gathered[USED].astype(F32) + gathered[USED + 1].astype(F32)
    return (
        grad_rows[None, :, None],
        gate_grads[None],
        up_grads[None],
        down_grads[None],
        gain_grads[None],
    )


def solution(mesh):
    grid = Mesh(mesh.devices.reshape(NZ, NY, NC, NS), ("z", "y", "core", "section"))
    return jax.shard_map(
        on_device,
        mesh=grid,
        in_specs=(
            P("section", None, DP, None),
            P(None, DP, None),
            P("section", DP, None),
            P("section", DP, None),
            P("section", DP, None),
            P("section", None),
            P(),
        ),
        out_specs=(
            P("section", None, DP, None),
            P("section", DP, None),
            P("section", DP, None),
            P("section", DP, None),
            P("section", None),
        ),
        check_vma=False,
    )
```

```python
import jax
import jax.numpy as jnp
from jax import lax
from jax.sharding import Mesh
from jax.sharding import PartitionSpec as P

NZ, NY, NC, NS = 8, 4, 2, 4
DP = ("z", "y", "core")
PLANE = ("z", "y")
LIVE = 85
GROUP = 24
USED = 22
ROWS = NY * GROUP
BF = jnp.bfloat16
F32 = jnp.float32


def dot_nt(a, b):
    return lax.dot_general(a, b, (((1,), (1,)), ((), ())), preferred_element_type=F32)


def dot_nn(a, b):
    return lax.dot_general(a, b, (((1,), (0,)), ((), ())), preferred_element_type=F32)


def dot_tn(a, b):
    return lax.dot_general(a, b, (((0,), (0,)), ((), ())), preferred_element_type=F32)


def row_of(micro, slot):
    position = jnp.where(micro == 0, slot, LIVE - 1 - slot)
    return GROUP * (position // USED) + position % USED


def swap_core(x):
    return lax.ppermute(x, "core", [(0, 1), (1, 0)])


def exchange(x):
    return lax.all_to_all(x, PLANE, 0, 0, tiled=True)


def spread_rows(own):
    count, half = own.shape
    along_z = lax.all_to_all(jnp.broadcast_to(own[None], (NZ, count, half)), "z", 0, 0, tiled=True)
    shifted = [along_z]
    for by in (1, 3, 2):
        shifted.append(lax.ppermute(along_z, "y", [(i, (i + by) % NY) for i in range(NY)]))
    swapped = [swap_core(x) for x in shifted]
    join = lambda xs: jnp.concatenate([x.reshape(NZ * count, half) for x in xs], axis=0)
    return join(shifted), join(swapped)


def selection(counts, y, core):
    shape = (2, 2, ROWS, NY, NZ, 8)
    at = lambda dim: lax.broadcasted_iota(jnp.int32, shape, dim)
    kind, part, row, shift, z, piece = (at(d) for d in range(6))
    by = jnp.where(shift == 0, 0, jnp.where(shift == 1, 1, jnp.where(shift == 2, 3, 2)))
    slot = z * NY * NC + ((y - by + NY) % NY) * NC + core
    micro = (piece // 2) % 2
    limit = jnp.where(micro == 0, counts[0], counts[1])
    hit = (row_of(micro, slot) == row) & (slot < limit) & (piece // 4 == kind) & (piece % 2 == part)
    return hit.astype(BF).reshape(4 * ROWS, NY * NZ * 8)


def gather_rows(hidden, top, counts, y, core):
    half = hidden.shape[-1] // 2
    own = jnp.concatenate([hidden, top], axis=0).reshape(8, half)
    pick_own = lax.optimization_barrier(selection(counts, y, core))
    pick_other = lax.optimization_barrier(selection(counts, y, 1 - core))
    mine, other = spread_rows(own)
    rows = (dot_nn(pick_own, mine) + dot_nn(pick_other, other)).astype(BF).reshape(2, 2, ROWS, half)
    return jnp.concatenate([rows[0, 0], rows[0, 1]], axis=1), rows[1, 0], rows[1, 1]


def wanted_rows(counts, y):
    shape = (NZ, NY, 8, GROUP)
    to_z, to_y, piece, row = (lax.broadcasted_iota(jnp.int32, shape, d) for d in range(4))
    slot = to_z * NY * NC + to_y * NC + piece // 2
    micro = piece % 2
    limit = jnp.where(micro == 0, counts[0], counts[1])
    hit = (piece < 4) & (row_of(micro, slot) == y * GROUP + row) & (slot < limit)
    carry = (y == 0) & ((piece == 4) & (row == USED) | (piece == 5) & (row == USED + 1))
    return (hit | carry).astype(BF).reshape(NZ * NY * 8, GROUP)


def on_device(hidden_in, grad_out, weight_gate, weight_up, weight_down, gain, counts):
    gate_mat, up_mat, down_mat = weight_gate[0], weight_up[0], weight_down[0]
    gain_row = gain[0]
    width = gate_mat.shape[1]
    half = width // 2
    lanes = width // (NC * NZ)
    z, y, core = lax.axis_index("z"), lax.axis_index("y"), lax.axis_index("core")
    section = lax.axis_index("section")

    def halves(x):
        return (
            lax.dynamic_slice_in_dim(x, core * half, half, 1),
            lax.dynamic_slice_in_dim(x, (1 - core) * half, half, 1),
        )

    units = gate_mat.shape[0]
    padded = -(-units // 256) * 256

    def pad_units(x, axis):
        widths = [(0, 0), (0, 0)]
        widths[axis] = (0, padded - units)
        return jnp.pad(x, widths)

    both = jnp.concatenate([pad_units(gate_mat, 0), pad_units(up_mat, 0)], axis=0)
    both_own, both_away = lax.optimization_barrier(halves(both))
    down_own, down_away = lax.optimization_barrier(halves(pad_units(down_mat, 0)))

    hidden, top_low, top_high = gather_rows(hidden_in[0, :, 0], grad_out[:, 0], counts, y, core)
    values = hidden.astype(F32)
    inv_rms = lax.rsqrt(jnp.mean(values * values, axis=-1, keepdims=True) + 1e-05)
    normed = (values * inv_rms * gain_row).astype(BF)
    gate_pre = dot_nt(normed, gate_mat)
    up_pre = dot_nt(normed, up_mat)
    sig = jax.nn.sigmoid(gate_pre)
    silu = gate_pre * sig
    activation = (silu * up_pre).astype(BF)
    gate_factor = pad_units(up_pre * sig * (1.0 + gate_pre * (1.0 - sig)), 1)
    up_factor = pad_units(silu, 1)
    gate_pre, up_pre = pad_units(gate_pre, 1), pad_units(up_pre, 1)
    mine = jnp.where(core == 0, top_low, top_high)
    other = jnp.where(core == 0, top_high, top_low)

    def tile_of(x, start):
        rows = lax.dynamic_slice_in_dim(x, y * GROUP, GROUP, 0)
        return lax.dynamic_slice_in_dim(rows, start, lanes, 1)

    hidden_tile = tile_of(hidden, core * half + z * lanes).astype(F32)
    up_tile = tile_of(mine, z * lanes)
    inv_tile = lax.dynamic_slice_in_dim(inv_rms, y * GROUP, GROUP, 0)
    gain_tile = lax.dynamic_slice_in_dim(gain_row, core * half + z * lanes, lanes, 0)
    in_group = lax.broadcasted_iota(jnp.int32, (NY, GROUP, 1), 1)
    tile_row = lax.broadcasted_iota(jnp.int32, (GROUP, 1), 0)

    for step in range(NS):
        last = step == NS - 1
        grad_act = dot_nt(mine, down_own) + dot_nt(other, down_away)
        grad_gate = (grad_act * gate_factor).astype(BF)
        grad_up = (grad_act * up_factor).astype(BF)
        grads = jnp.concatenate([grad_gate, grad_up], axis=1)
        inner = jnp.sum(grad_gate.astype(F32) * gate_pre + grad_up.astype(F32) * up_pre, axis=1)
        inner = jnp.tile(jnp.pad(inner, (0, lanes - ROWS)), NZ)

        def partial_of(weights, start):
            partial = dot_nn(grads, weights)
            packed = jnp.where(in_group == USED, inner, partial.reshape(NY, GROUP, half))
            if last:
                scaled = lax.dynamic_slice_in_dim(values, start, half, 1) * inv_rms
                packed = jnp.where(in_group == USED + 1, jnp.sum(partial * scaled, axis=0), packed)
            return packed.astype(BF)

        away = swap_core(partial_of(both_away, (1 - core) * half))
        kept = partial_of(both_own, core * half)
        summed = (kept.astype(F32) + away.astype(F32)).astype(BF)
        pieces = summed.reshape(NY, GROUP, NZ, lanes).transpose(2, 0, 1, 3).reshape(NZ * NY, GROUP, lanes)
        total = jnp.sum(exchange(pieces).astype(F32), axis=0)
        row_sum = lax.dynamic_slice_in_dim(total[USED], y * GROUP, GROUP, 0)[:, None]
        grad_tile = (
            up_tile.astype(F32)
            + inv_tile * (gain_tile * total)
            - hidden_tile * inv_tile * inv_tile * row_sum / width
        )
        grad_tile = jnp.where(tile_row < USED, grad_tile, 0.0).astype(BF)
        if last:
            gain_sum = total[USED + 1]
            high = gain_sum.astype(BF)
            low = (gain_sum - high.astype(F32)).astype(BF)
            grad_tile = jnp.where(tile_row == USED, high, grad_tile)
            grad_tile = jnp.where(tile_row == USED + 1, low, grad_tile)
            wanted = lax.optimization_barrier(wanted_rows(counts, y))
            sent = dot_nn(wanted, grad_tile).astype(BF).reshape(NZ * NY, 8, lanes)
            spread = exchange(sent)
            gate_grads = dot_tn(grad_gate[:, :units], normed).astype(BF)
            up_grads = dot_tn(grad_up[:, :units], normed).astype(BF)
            upstream = jnp.concatenate(
                [jnp.where(core == 0, mine, other), jnp.where(core == 0, other, mine)], axis=1
            )
            down_grads = dot_tn(activation, upstream).astype(BF)
            spread, gate_grads, up_grads, down_grads = lax.optimization_barrier(
                (spread, gate_grads, up_grads, down_grads)
            )
            from_mine = jnp.sum(spread.reshape(NZ, NY, 8, lanes).astype(F32), axis=1).astype(BF)
            from_mine = from_mine.transpose(1, 0, 2).reshape(8, half)
            from_other = swap_core(from_mine)
            break
        moved = lax.ppermute(grad_tile, "section", [(NS - 1 - step, NS - 2 - step)])
        grad_tile = jnp.where(section == NS - 2 - step, moved, up_tile)
        spread = exchange(jnp.broadcast_to(grad_tile[None], (NZ * NY, GROUP, lanes)))
        arrived = swap_core(spread)

        def unpack(x):
            return x.reshape(NZ, NY, GROUP, lanes).transpose(1, 2, 0, 3).reshape(ROWS, half)

        mine, other = unpack(spread), unpack(arrived)
        up_tile = grad_tile

    final = jnp.concatenate(
        [jnp.where(core == 0, from_mine, from_other), jnp.where(core == 0, from_other, from_mine)], axis=1
    )
    own_pair = jnp.where(core == 0, final[0:2], final[2:4])
    gain_grads = final[4].astype(F32) + final[5].astype(F32)
    return (
        own_pair[None, :, None],
        gate_grads[None],
        up_grads[None],
        down_grads[None],
        gain_grads[None],
    )


def solution(mesh):
    grid = Mesh(mesh.devices.reshape(NZ, NY, NC, NS), ("z", "y", "core", "section"))
    return jax.shard_map(
        on_device,
        mesh=grid,
        in_specs=(
            P("section", None, DP, None),
            P(None, DP, None),
            P("section", DP, None),
            P("section", DP, None),
            P("section", DP, None),
            P("section", None),
            P(),
        ),
        out_specs=(
            P("section", None, DP, None),
            P("section", DP, None),
            P("section", DP, None),
            P("section", DP, None),
            P("section", None),
        ),
        check_vma=False,
    )
```

```python
import jax
import jax.numpy as jnp
from jax import lax
from jax.sharding import Mesh
from jax.sharding import PartitionSpec as P

NZ, NY, NC, NS = 8, 4, 2, 4
DP = ("z", "y", "core")
PLANE = ("z", "y")
LIVE = 85
GROUP = 24
USED = 22
ROWS = NY * GROUP
BF = jnp.bfloat16
F32 = jnp.float32


def dot_nt(a, b):
    return lax.dot_general(a, b, (((1,), (1,)), ((), ())), preferred_element_type=F32)


def dot_nn(a, b):
    return lax.dot_general(a, b, (((1,), (0,)), ((), ())), preferred_element_type=F32)


def dot_tn(a, b):
    return lax.dot_general(a, b, (((0,), (0,)), ((), ())), preferred_element_type=F32)


def row_of(micro, slot):
    position = jnp.where(micro == 0, slot, LIVE - 1 - slot)
    return GROUP * (position // USED) + position % USED


def swap_core(x):
    return lax.ppermute(x, "core", [(0, 1), (1, 0)])


def exchange(x):
    return lax.all_to_all(x, PLANE, 0, 0, tiled=True)


def spread_rows(own):
    count, half = own.shape
    along_z = lax.all_to_all(jnp.broadcast_to(own[None], (NZ, count, half)), "z", 0, 0, tiled=True)
    shifted = [along_z]
    for by in (1, 3, 2):
        shifted.append(lax.ppermute(along_z, "y", [(i, (i + by) % NY) for i in range(NY)]))
    swapped = [swap_core(x) for x in shifted]
    join = lambda xs: jnp.concatenate([x.reshape(NZ * count, half) for x in xs], axis=0)
    return join(shifted), join(swapped)


def selection(counts, y, core):
    shape = (2, 2, ROWS, NY, NZ, 8)
    at = lambda dim: lax.broadcasted_iota(jnp.int32, shape, dim)
    kind, part, row, shift, z, piece = (at(d) for d in range(6))
    by = jnp.where(shift == 0, 0, jnp.where(shift == 1, 1, jnp.where(shift == 2, 3, 2)))
    slot = z * NY * NC + ((y - by + NY) % NY) * NC + core
    micro = (piece // 2) % 2
    limit = jnp.where(micro == 0, counts[0], counts[1])
    hit = (row_of(micro, slot) == row) & (slot < limit) & (piece // 4 == kind) & (piece % 2 == part)
    return hit.astype(BF).reshape(4 * ROWS, NY * NZ * 8)


def gather_rows(hidden, top, counts, y, core):
    half = hidden.shape[-1] // 2
    own = jnp.concatenate([hidden, top], axis=0).reshape(8, half)
    pick_own, pick_other, wanted = lax.optimization_barrier(
        (selection(counts, y, core), selection(counts, y, 1 - core), wanted_rows(counts, y))
    )
    mine, other = spread_rows(own)
    rows = (dot_nn(pick_own, mine) + dot_nn(pick_other, other)).astype(BF).reshape(2, 2, ROWS, half)
    return jnp.concatenate([rows[0, 0], rows[0, 1]], axis=1), rows[1, 0], rows[1, 1], wanted


def wanted_rows(counts, y):
    shape = (NZ * NY * 8, GROUP)
    index, row = (lax.broadcasted_iota(jnp.int32, shape, d) for d in range(2))
    place, piece = index // 8, index % 8
    slot = place * NC + piece // 2
    micro = piece % 2
    limit = jnp.where(micro == 0, counts[0], counts[1])
    hit = (piece < 4) & (row_of(micro, slot) == y * GROUP + row) & (slot < limit)
    carry = (y == 0) & ((piece == 4) & (row == USED) | (piece == 5) & (row == USED + 1))
    return (hit | carry).astype(BF)


def on_device(hidden_in, grad_out, weight_gate, weight_up, weight_down, gain, counts):
    gate_mat, up_mat, down_mat = weight_gate[0], weight_up[0], weight_down[0]
    gain_row = gain[0]
    width = gate_mat.shape[1]
    half = width // 2
    lanes = width // (NC * NZ)
    z, y, core = lax.axis_index("z"), lax.axis_index("y"), lax.axis_index("core")
    section = lax.axis_index("section")

    def halves(x):
        return (
            lax.dynamic_slice_in_dim(x, core * half, half, 1),
            lax.dynamic_slice_in_dim(x, (1 - core) * half, half, 1),
        )

    units = gate_mat.shape[0]
    padded = -(-units // 256) * 256

    def pad_units(x, axis):
        widths = [(0, 0), (0, 0)]
        widths[axis] = (0, padded - units)
        return jnp.pad(x, widths)

    gate_own, gate_away = halves(gate_mat)
    up_own, up_away = halves(up_mat)
    both_own = jnp.concatenate([pad_units(gate_own, 0), pad_units(up_own, 0)], axis=0)
    both_away = jnp.concatenate([pad_units(gate_away, 0), pad_units(up_away, 0)], axis=0)
    down_own, down_away = (pad_units(x, 0) for x in halves(down_mat))
    both_own, both_away, down_own, down_away = lax.optimization_barrier(
        (both_own, both_away, down_own, down_away)
    )

    hidden, top_low, top_high, wanted = gather_rows(hidden_in[0, :, 0], grad_out[:, 0], counts, y, core)
    values = hidden.astype(F32)
    inv_rms = lax.rsqrt(jnp.mean(values * values, axis=-1, keepdims=True) + 1e-05)
    normed = (values * inv_rms * gain_row).astype(BF)
    gate_pre = dot_nt(normed, gate_mat)
    up_pre = dot_nt(normed, up_mat)
    sig = jax.nn.sigmoid(gate_pre)
    silu = gate_pre * sig
    activation = (silu * up_pre).astype(BF)
    gate_factor = pad_units(up_pre * sig * (1.0 + gate_pre * (1.0 - sig)), 1)
    up_factor = pad_units(silu, 1)
    gate_pre, up_pre = pad_units(gate_pre, 1), pad_units(up_pre, 1)
    mine = jnp.where(core == 0, top_low, top_high)
    other = jnp.where(core == 0, top_high, top_low)

    def tile_of(x, start):
        rows = lax.dynamic_slice_in_dim(x, y * GROUP, GROUP, 0)
        return lax.dynamic_slice_in_dim(rows, start, lanes, 1)

    hidden_tile = tile_of(hidden, core * half + z * lanes).astype(F32)
    up_tile = tile_of(mine, z * lanes)
    inv_tile = lax.dynamic_slice_in_dim(inv_rms, y * GROUP, GROUP, 0)
    gain_tile = lax.dynamic_slice_in_dim(gain_row, core * half + z * lanes, lanes, 0)
    in_group = lax.broadcasted_iota(jnp.int32, (NY, GROUP, 1), 1)
    tile_row = lax.broadcasted_iota(jnp.int32, (GROUP, 1), 0)

    for step in range(NS):
        last = step == NS - 1
        grad_act = dot_nt(mine, down_own) + dot_nt(other, down_away)
        grad_gate = (grad_act * gate_factor).astype(BF)
        grad_up = (grad_act * up_factor).astype(BF)
        grads = jnp.concatenate([grad_gate, grad_up], axis=1)
        inner = jnp.sum(grad_gate.astype(F32) * gate_pre + grad_up.astype(F32) * up_pre, axis=1)
        inner = jnp.tile(jnp.pad(inner, (0, lanes - ROWS)), NZ)

        def partial_of(weights, start):
            partial = dot_nn(grads, weights)
            packed = jnp.where(in_group == USED, inner, partial.reshape(NY, GROUP, half))
            if last:
                scaled = lax.dynamic_slice_in_dim(values, start, half, 1) * inv_rms
                packed = jnp.where(in_group == USED + 1, jnp.sum(partial * scaled, axis=0), packed)
            return packed.astype(BF)

        away = swap_core(partial_of(both_away, (1 - core) * half))
        kept = partial_of(both_own, core * half)
        summed = (kept.astype(F32) + away.astype(F32)).astype(BF)
        pieces = summed.reshape(NY, GROUP, NZ, lanes).transpose(2, 0, 1, 3).reshape(NZ * NY, GROUP, lanes)
        if last:
            pieces, grad_gate, grad_up, mine, other = lax.optimization_barrier(
                (pieces, grad_gate, grad_up, mine, other)
            )
        total = jnp.sum(exchange(pieces).astype(F32), axis=0)
        row_sum = lax.dynamic_slice_in_dim(total[USED], y * GROUP, GROUP, 0)[:, None]
        grad_tile = (
            up_tile.astype(F32)
            + inv_tile * (gain_tile * total)
            - hidden_tile * inv_tile * inv_tile * row_sum / width
        )
        grad_tile = jnp.where(tile_row < USED, grad_tile, 0.0).astype(BF)
        if last:
            gain_sum = total[USED + 1]
            high = gain_sum.astype(BF)
            low = (gain_sum - high.astype(F32)).astype(BF)
            grad_tile = jnp.where(tile_row == USED, high, grad_tile)
            grad_tile = jnp.where(tile_row == USED + 1, low, grad_tile)
            sent = dot_nn(wanted, grad_tile).astype(BF).reshape(NZ * NY, 8, lanes)
            spread = exchange(sent)
            gate_grads = dot_tn(grad_gate[:, :units], normed).astype(BF)
            up_grads = dot_tn(grad_up[:, :units], normed).astype(BF)
            upstream = jnp.concatenate(
                [jnp.where(core == 0, mine, other), jnp.where(core == 0, other, mine)], axis=1
            )
            down_grads = dot_tn(activation, upstream).astype(BF)
            spread, gate_grads, up_grads, down_grads = lax.optimization_barrier(
                (spread, gate_grads, up_grads, down_grads)
            )
            from_mine = jnp.sum(spread.reshape(NZ, NY, 8, lanes).astype(F32), axis=1).astype(BF)
            from_mine = from_mine.transpose(1, 0, 2).reshape(8, half)
            from_other = swap_core(from_mine)
            break
        moved = lax.ppermute(grad_tile, "section", [(NS - 1 - step, NS - 2 - step)])
        grad_tile = jnp.where(section == NS - 2 - step, moved, up_tile)
        spread = exchange(jnp.broadcast_to(grad_tile[None], (NZ * NY, GROUP, lanes)))
        arrived = swap_core(spread)

        def unpack(x):
            return x.reshape(NZ, NY, GROUP, lanes).transpose(1, 2, 0, 3).reshape(ROWS, half)

        mine, other = unpack(spread), unpack(arrived)
        up_tile = grad_tile

    final = jnp.concatenate(
        [jnp.where(core == 0, from_mine, from_other), jnp.where(core == 0, from_other, from_mine)], axis=1
    )
    own_pair = jnp.where(core == 0, final[0:2], final[2:4])
    gain_grads = final[4].astype(F32) + final[5].astype(F32)
    return (
        own_pair[None, :, None],
        gate_grads[None],
        up_grads[None],
        down_grads[None],
        gain_grads[None],
    )


def solution(mesh):
    grid = Mesh(mesh.devices.reshape(NZ, NY, NC, NS), ("z", "y", "core", "section"))
    return jax.shard_map(
        on_device,
        mesh=grid,
        in_specs=(
            P("section", None, DP, None),
            P(None, DP, None),
            P("section", DP, None),
            P("section", DP, None),
            P("section", DP, None),
            P("section", None),
            P(),
        ),
        out_specs=(
            P("section", None, DP, None),
            P("section", DP, None),
            P("section", DP, None),
            P("section", DP, None),
            P("section", None),
        ),
        check_vma=False,
    )
```

```python
import jax
import jax.numpy as jnp
from jax import lax
from jax.sharding import Mesh
from jax.sharding import PartitionSpec as P

NZ, NY, NC, NS = 8, 4, 2, 4
DP = ("z", "y", "core")
PLANE = ("z", "y")
LIVE = 85
GROUP = 24
USED = 22
ROWS = NY * GROUP
BF = jnp.bfloat16
F32 = jnp.float32


def dot_nt(a, b):
    return lax.dot_general(a, b, (((1,), (1,)), ((), ())), preferred_element_type=F32)


def dot_nn(a, b):
    return lax.dot_general(a, b, (((1,), (0,)), ((), ())), preferred_element_type=F32)


def dot_tn(a, b):
    return lax.dot_general(a, b, (((0,), (0,)), ((), ())), preferred_element_type=F32)


def row_of(micro, slot):
    position = jnp.where(micro == 0, slot, LIVE - 1 - slot)
    return GROUP * (position // USED) + position % USED


def swap_core(x):
    return lax.ppermute(x, "core", [(0, 1), (1, 0)])


def exchange(x):
    return lax.all_to_all(x, PLANE, 0, 0, tiled=True)


def spread_rows(own, weights):
    count, half = own.shape
    along_z = lax.all_to_all(jnp.broadcast_to(own[None], (NZ, count, half)), "z", 0, 0, tiled=True)
    along_z, weights = lax.optimization_barrier((along_z, weights))
    shifted = [along_z]
    for by in (1, 3, 2):
        shifted.append(lax.ppermute(along_z, "y", [(i, (i + by) % NY) for i in range(NY)]))
    swapped = [swap_core(x) for x in shifted]
    join = lambda xs: jnp.concatenate([x.reshape(NZ * count, half) for x in xs], axis=0)
    return join(shifted), join(swapped), weights


def selection(counts, y, core, first_half):
    shape = (2, 2, ROWS, NY, NZ, 8)
    at = lambda dim: lax.broadcasted_iota(jnp.int32, shape, dim)
    kind, part, row, shift, z, piece = (at(d) for d in range(6))
    by = jnp.where(shift == 0, 0, jnp.where(shift == 1, 1, jnp.where(shift == 2, 3, 2)))
    slot = z * NY * NC + ((y - by + NY) % NY) * NC + core
    micro = (piece // 2) % 2
    limit = jnp.where(micro == 0, counts[0], counts[1])
    hit = (row_of(micro, slot) == row) & (slot < limit) & (piece // 4 == kind) & (piece % 2 == (part ^ first_half))
    return hit.astype(BF).reshape(4 * ROWS, NY * NZ * 8)


def gather_rows(hidden, top, weights, counts, y, core):
    half = hidden.shape[-1] // 2
    own = jnp.concatenate([hidden, top], axis=0).reshape(8, half)
    pick_own, pick_other, wanted = lax.optimization_barrier(
        (selection(counts, y, core, core), selection(counts, y, 1 - core, core), wanted_rows(counts, y))
    )
    mine, other, weights = spread_rows(own, weights)
    rows = (dot_nn(pick_own, mine) + dot_nn(pick_other, other)).astype(BF).reshape(2, 2, ROWS, half)
    return (rows[0, 0], rows[0, 1]), (rows[1, 0], rows[1, 1]), wanted, weights


def wanted_rows(counts, y):
    shape = (NZ * NY * 8, GROUP)
    index, row = (lax.broadcasted_iota(jnp.int32, shape, d) for d in range(2))
    place, piece = index // 8, index % 8
    slot = place * NC + piece // 2
    micro = piece % 2
    limit = jnp.where(micro == 0, counts[0], counts[1])
    hit = (piece < 4) & (row_of(micro, slot) == y * GROUP + row) & (slot < limit)
    carry = (y == 0) & ((piece == 4) & (row == USED) | (piece == 5) & (row == USED + 1))
    return (hit | carry).astype(BF)


def on_device(hidden_in, grad_out, weight_gate, weight_up, weight_down, gain, counts):
    gate_mat, up_mat, down_mat = weight_gate[0], weight_up[0], weight_down[0]
    gain_row = gain[0]
    width = gate_mat.shape[1]
    half = width // 2
    lanes = width // (NC * NZ)
    z, y, core = lax.axis_index("z"), lax.axis_index("y"), lax.axis_index("core")
    section = lax.axis_index("section")

    def halves(x):
        return (
            lax.dynamic_slice_in_dim(x, core * half, half, 1),
            lax.dynamic_slice_in_dim(x, (1 - core) * half, half, 1),
        )

    def whole(own, away):
        return jnp.concatenate(
            [jnp.where(core == 0, own, away), jnp.where(core == 0, away, own)], axis=1
        )

    units = gate_mat.shape[0]
    padded = -(-units // 256) * 256

    def pad_units(x):
        return jnp.pad(x, ((0, padded - units), (0, 0)))

    hidden, (mine, other), wanted, (gate_mat, up_mat, down_mat) = gather_rows(
        hidden_in[0, :, 0], grad_out[:, 0], (gate_mat, up_mat, down_mat), counts, y, core
    )
    gate_own, gate_away = halves(gate_mat)
    up_own, up_away = halves(up_mat)
    both_own = jnp.concatenate([pad_units(gate_own), pad_units(up_own)], axis=0)
    both_away = jnp.concatenate([pad_units(gate_away), pad_units(up_away)], axis=0)
    down_own, down_away = (pad_units(x) for x in halves(down_mat))
    both_own, both_away, down_own, down_away = lax.optimization_barrier(
        (both_own, both_away, down_own, down_away)
    )

    values = [x.astype(F32) for x in hidden]
    squares = sum(jnp.sum(x * x, axis=-1, keepdims=True) for x in values)
    inv_rms = lax.rsqrt(squares / width + 1e-05)
    gain_halves = halves(gain_row[None])
    unit_own, unit_away = (x * inv_rms for x in values)
    normed_own = (unit_own * gain_halves[0]).astype(BF)
    normed_away = (unit_away * gain_halves[1]).astype(BF)
    pre = dot_nt(normed_own, both_own) + dot_nt(normed_away, both_away)
    gate_pre, up_pre = pre[:, :padded], pre[:, padded:]
    sig = jax.nn.sigmoid(gate_pre)
    up_factor = gate_pre * sig
    activation = (up_factor * up_pre).astype(BF)
    gate_factor = up_pre * sig * (1.0 + gate_pre * (1.0 - sig))

    def tile_of(x):
        rows = lax.dynamic_slice_in_dim(x, y * GROUP, GROUP, 0)
        return lax.dynamic_slice_in_dim(rows, z * lanes, lanes, 1)

    hidden_tile = tile_of(hidden[0]).astype(F32)
    up_tile = tile_of(mine)
    inv_tile = lax.dynamic_slice_in_dim(inv_rms, y * GROUP, GROUP, 0)
    gain_tile = lax.dynamic_slice_in_dim(gain_row, core * half + z * lanes, lanes, 0)
    in_group = lax.broadcasted_iota(jnp.int32, (NY, GROUP, 1), 1)
    tile_row = lax.broadcasted_iota(jnp.int32, (GROUP, 1), 0)

    for step in range(NS):
        last = step == NS - 1
        grad_act = dot_nt(mine, down_own) + dot_nt(other, down_away)
        grad_gate = (grad_act * gate_factor).astype(BF)
        grad_up = (grad_act * up_factor).astype(BF)
        grads = jnp.concatenate([grad_gate, grad_up], axis=1)
        inner = jnp.sum(grad_gate.astype(F32) * gate_pre + grad_up.astype(F32) * up_pre, axis=1)
        inner = jnp.tile(jnp.pad(inner, (0, lanes - ROWS)), NZ)

        def partial_of(weights, unit_rows):
            partial = dot_nn(grads, weights)
            packed = jnp.where(in_group == USED, inner, partial.reshape(NY, GROUP, half))
            if last:
                packed = jnp.where(in_group == USED + 1, jnp.sum(partial * unit_rows, axis=0), packed)
            return packed.astype(BF)

        away = swap_core(partial_of(both_away, unit_away))
        kept = partial_of(both_own, unit_own)
        summed = (kept.astype(F32) + away.astype(F32)).astype(BF)
        pieces = summed.reshape(NY, GROUP, NZ, lanes).transpose(2, 0, 1, 3).reshape(NZ * NY, GROUP, lanes)
        if last:
            pieces, grad_gate, grad_up, mine, other = lax.optimization_barrier(
                (pieces, grad_gate, grad_up, mine, other)
            )
        total = jnp.sum(exchange(pieces).astype(F32), axis=0)
        row_sum = lax.dynamic_slice_in_dim(total[USED], y * GROUP, GROUP, 0)[:, None]
        grad_tile = (
            up_tile.astype(F32)
            + inv_tile * (gain_tile * total)
            - hidden_tile * inv_tile * inv_tile * row_sum / width
        )
        grad_tile = jnp.where(tile_row < USED, grad_tile, 0.0).astype(BF)
        if last:
            gain_sum = total[USED + 1]
            high = gain_sum.astype(BF)
            low = (gain_sum - high.astype(F32)).astype(BF)
            grad_tile = jnp.where(tile_row == USED, high, grad_tile)
            grad_tile = jnp.where(tile_row == USED + 1, low, grad_tile)
            sent = dot_nn(wanted, grad_tile).astype(BF).reshape(NZ * NY, 8, lanes)
            spread = exchange(sent)
            normed = whole(normed_own, normed_away)
            gate_grads = dot_tn(grad_gate[:, :units], normed).astype(BF)
            up_grads = dot_tn(grad_up[:, :units], normed).astype(BF)
            down_grads = dot_tn(activation[:, :units], whole(mine, other)).astype(BF)
            spread, gate_grads, up_grads, down_grads = lax.optimization_barrier(
                (spread, gate_grads, up_grads, down_grads)
            )
            from_mine = jnp.sum(spread.reshape(NZ, NY, 8, lanes).astype(F32), axis=1).astype(BF)
            from_mine = from_mine.transpose(1, 0, 2).reshape(8, half)
            from_other = swap_core(from_mine)
            break
        moved = lax.ppermute(grad_tile, "section", [(NS - 1 - step, NS - 2 - step)])
        grad_tile = jnp.where(section == NS - 2 - step, moved, up_tile)
        spread = exchange(jnp.broadcast_to(grad_tile[None], (NZ * NY, GROUP, lanes)))
        arrived = swap_core(spread)

        def unpack(x):
            return x.reshape(NZ, NY, GROUP, lanes).transpose(1, 2, 0, 3).reshape(ROWS, half)

        mine, other = unpack(spread), unpack(arrived)
        up_tile = grad_tile

    final = whole(from_mine, from_other)
    own_pair = jnp.where(core == 0, final[0:2], final[2:4])
    gain_grads = final[4].astype(F32) + final[5].astype(F32)
    return (
        own_pair[None, :, None],
        gate_grads[None],
        up_grads[None],
        down_grads[None],
        gain_grads[None],
    )


def solution(mesh):
    grid = Mesh(mesh.devices.reshape(NZ, NY, NC, NS), ("z", "y", "core", "section"))
    return jax.shard_map(
        on_device,
        mesh=grid,
        in_specs=(
            P("section", None, DP, None),
            P(None, DP, None),
            P("section", DP, None),
            P("section", DP, None),
            P("section", DP, None),
            P("section", None),
            P(),
        ),
        out_specs=(
            P("section", None, DP, None),
            P("section", DP, None),
            P("section", DP, None),
            P("section", DP, None),
            P("section", None),
        ),
        check_vma=False,
    )
```

```python
import jax
import jax.numpy as jnp
from jax import lax
from jax.sharding import Mesh
from jax.sharding import PartitionSpec as P

NZ, NY, NC, NS = 8, 4, 2, 4
DP = ("z", "y", "core")
PLANE = ("z", "y")
LIVE = 85
PACK = 12
GROUP = 24
USED = 22
ROWS = NY * GROUP
BF = jnp.bfloat16
F32 = jnp.float32


def dot_nt(a, b):
    return lax.dot_general(a, b, (((1,), (1,)), ((), ())), preferred_element_type=F32)


def dot_nn(a, b):
    return lax.dot_general(a, b, (((1,), (0,)), ((), ())), preferred_element_type=F32)


def dot_tn(a, b):
    return lax.dot_general(a, b, (((0,), (0,)), ((), ())), preferred_element_type=F32)


def row_of(micro, slot):
    position = jnp.where(micro == 0, slot, LIVE - 1 - slot)
    return GROUP * (position // USED) + position % USED


def swap_core(x):
    return lax.ppermute(x, "core", [(0, 1), (1, 0)])


def exchange(x):
    return lax.all_to_all(x, PLANE, 0, 0, tiled=True)


def packed_slot(counts, index, residue):
    first = jnp.clip((counts[0] - residue + NY * NC - 1) // (NY * NC), 0, NZ)
    micro = (index >= first).astype(jnp.int32)
    at_z = index - first * micro
    slot = at_z * NY * NC + residue
    return micro, at_z, slot, slot < jnp.where(micro == 0, counts[0], counts[1])


def packing(counts, y, core):
    shape = (4, PACK, NZ, 8)
    kind_half, index, z, piece = (lax.broadcasted_iota(jnp.int32, shape, d) for d in range(4))
    micro, at_z, _, live = packed_slot(counts, index, y * NC + core)
    hit = live & (at_z == z) & (piece == (kind_half // 2) * 4 + micro * 2 + kind_half % 2)
    return hit.astype(BF).reshape(4 * PACK, NZ * 8)


def spread_rows(own, weights, pack):
    count, half = own.shape
    along_z = lax.all_to_all(jnp.broadcast_to(own[None], (NZ, count, half)), "z", 0, 0, tiled=True)
    along_z, weights = lax.optimization_barrier((along_z, weights))
    packed = dot_nn(pack, along_z.reshape(NZ * count, half)).astype(BF)
    shifted = [packed]
    for by in (1, 3, 2):
        shifted.append(lax.ppermute(packed, "y", [(i, (i + by) % NY) for i in range(NY)]))
    swapped = [swap_core(x) for x in shifted]
    return jnp.concatenate(shifted, axis=0), jnp.concatenate(swapped, axis=0), weights


def selection(counts, y, core, first_half):
    shape = (4, ROWS, NY, 4, PACK)
    out, row, shift, kind_half, index = (lax.broadcasted_iota(jnp.int32, shape, d) for d in range(5))
    by = jnp.where(shift == 0, 0, jnp.where(shift == 1, 1, jnp.where(shift == 2, 3, 2)))
    micro, _, slot, live = packed_slot(counts, index, ((y - by + NY) % NY) * NC + core)
    hit = live & (row_of(micro, slot) == row) & (kind_half == (out ^ first_half))
    return hit.astype(BF).reshape(4 * ROWS, NY * 4 * PACK)


def gather_rows(hidden, top, weights, counts, y, core):
    half = hidden.shape[-1] // 2
    own = jnp.concatenate([hidden, top], axis=0).reshape(8, half)
    pack, pick_own, pick_other, wanted = lax.optimization_barrier(
        (
            packing(counts, y, core),
            selection(counts, y, core, core),
            selection(counts, y, 1 - core, core),
            wanted_rows(counts, y),
        )
    )
    mine, other, weights = spread_rows(own, weights, pack)
    rows = (dot_nn(pick_own, mine) + dot_nn(pick_other, other)).astype(BF).reshape(2, 2, ROWS, half)
    return (rows[0, 0], rows[0, 1]), (rows[1, 0], rows[1, 1]), wanted, weights


def wanted_rows(counts, y):
    shape = (NZ * NY * 8, GROUP)
    index, row = (lax.broadcasted_iota(jnp.int32, shape, d) for d in range(2))
    place, piece = index // 8, index % 8
    slot = place * NC + piece // 2
    micro = piece % 2
    limit = jnp.where(micro == 0, counts[0], counts[1])
    hit = (piece < 4) & (row_of(micro, slot) == y * GROUP + row) & (slot < limit)
    carry = (y == 0) & ((piece == 4) & (row == USED) | (piece == 5) & (row == USED + 1))
    return (hit | carry).astype(BF)


def on_device(hidden_in, grad_out, weight_gate, weight_up, weight_down, gain, counts):
    gate_mat, up_mat, down_mat = weight_gate[0], weight_up[0], weight_down[0]
    gain_row = gain[0]
    width = gate_mat.shape[1]
    half = width // 2
    lanes = width // (NC * NZ)
    z, y, core = lax.axis_index("z"), lax.axis_index("y"), lax.axis_index("core")
    section = lax.axis_index("section")

    def halves(x):
        return (
            lax.dynamic_slice_in_dim(x, core * half, half, 1),
            lax.dynamic_slice_in_dim(x, (1 - core) * half, half, 1),
        )

    def whole(own, away):
        return jnp.concatenate(
            [jnp.where(core == 0, own, away), jnp.where(core == 0, away, own)], axis=1
        )

    def unpack(x):
        return x.reshape(NZ, NY, GROUP, lanes).transpose(1, 2, 0, 3).reshape(ROWS, half)

    units = gate_mat.shape[0]
    padded = -(-units // 256) * 256

    def pad_units(x):
        return jnp.pad(x, ((0, padded - units), (0, 0)))

    hidden, (mine, other), wanted, (gate_mat, up_mat, down_mat) = gather_rows(
        hidden_in[0, :, 0], grad_out[:, 0], (gate_mat, up_mat, down_mat), counts, y, core
    )
    gate_own, gate_away = halves(gate_mat)
    up_own, up_away = halves(up_mat)
    both_own = jnp.concatenate([pad_units(gate_own), pad_units(up_own)], axis=0)
    both_away = jnp.concatenate([pad_units(gate_away), pad_units(up_away)], axis=0)
    down_own, down_away = (pad_units(x) for x in halves(down_mat))
    both_own, both_away, down_own, down_away = lax.optimization_barrier(
        (both_own, both_away, down_own, down_away)
    )

    values = [x.astype(F32) for x in hidden]
    squares = sum(jnp.sum(x * x, axis=-1, keepdims=True) for x in values)
    inv_rms = lax.rsqrt(squares / width + 1e-05)
    gain_halves = halves(gain_row[None])
    unit_own, unit_away = (x * inv_rms for x in values)
    normed_own = (unit_own * gain_halves[0]).astype(BF)
    normed_away = (unit_away * gain_halves[1]).astype(BF)
    pre = dot_nt(normed_own, both_own) + dot_nt(normed_away, both_away)
    gate_pre, up_pre = pre[:, :padded], pre[:, padded:]
    sig = jax.nn.sigmoid(gate_pre)
    up_factor = gate_pre * sig
    activation = (up_factor * up_pre).astype(BF)
    gate_factor = up_pre * sig * (1.0 + gate_pre * (1.0 - sig))

    def tile_of(x):
        rows = lax.dynamic_slice_in_dim(x, y * GROUP, GROUP, 0)
        return lax.dynamic_slice_in_dim(rows, z * lanes, lanes, 1)

    hidden_tile = tile_of(hidden[0]).astype(F32)
    up_tile = tile_of(mine)
    inv_tile = lax.dynamic_slice_in_dim(inv_rms, y * GROUP, GROUP, 0)
    gain_tile = lax.dynamic_slice_in_dim(gain_row, core * half + z * lanes, lanes, 0)
    in_group = lax.broadcasted_iota(jnp.int32, (NY, GROUP, 1), 1)
    tile_row = lax.broadcasted_iota(jnp.int32, (GROUP, 1), 0)

    for step in range(NS):
        last = step == NS - 1
        grad_act = dot_nt(mine, down_own) + dot_nt(other, down_away)
        grad_gate = (grad_act * gate_factor).astype(BF)
        grad_up = (grad_act * up_factor).astype(BF)
        grads = jnp.concatenate([grad_gate, grad_up], axis=1)
        inner = jnp.sum(grad_gate.astype(F32) * gate_pre + grad_up.astype(F32) * up_pre, axis=1)
        inner = jnp.tile(jnp.pad(inner, (0, lanes - ROWS)), NZ)

        def partial_of(weights, unit_rows):
            partial = dot_nn(grads, weights)
            packed = jnp.where(in_group == USED, inner, partial.reshape(NY, GROUP, half))
            if last:
                packed = jnp.where(in_group == USED + 1, jnp.sum(partial * unit_rows, axis=0), packed)
            return packed.astype(BF)

        away = swap_core(partial_of(both_away, unit_away))
        kept = partial_of(both_own, unit_own)
        summed = (kept.astype(F32) + away.astype(F32)).astype(BF)
        pieces = summed.reshape(NY, GROUP, NZ, lanes).transpose(2, 0, 1, 3).reshape(NZ * NY, GROUP, lanes)
        if last:
            pieces, grad_gate, grad_up, spread, arrived = lax.optimization_barrier(
                (pieces, grad_gate, grad_up, spread, arrived)
            )
            upstream = whole(unpack(spread), unpack(arrived))
        total = jnp.sum(exchange(pieces).astype(F32), axis=0)
        row_sum = lax.dynamic_slice_in_dim(total[USED], y * GROUP, GROUP, 0)[:, None]
        grad_tile = (
            up_tile.astype(F32)
            + inv_tile * (gain_tile * total)
            - hidden_tile * inv_tile * inv_tile * row_sum / width
        )
        grad_tile = jnp.where(tile_row < USED, grad_tile, 0.0).astype(BF)
        if last:
            gain_sum = total[USED + 1]
            high = gain_sum.astype(BF)
            low = (gain_sum - high.astype(F32)).astype(BF)
            grad_tile = jnp.where(tile_row == USED, high, grad_tile)
            grad_tile = jnp.where(tile_row == USED + 1, low, grad_tile)
            sent = dot_nn(wanted, grad_tile).astype(BF).reshape(NZ * NY, 8, lanes)
            spread = exchange(sent)
            normed = whole(normed_own, normed_away)
            gate_grads = dot_tn(grad_gate[:, :units], normed).astype(BF)
            up_grads = dot_tn(grad_up[:, :units], normed).astype(BF)
            down_grads = dot_tn(activation[:, :units], upstream).astype(BF)
            spread, gate_grads, up_grads, down_grads = lax.optimization_barrier(
                (spread, gate_grads, up_grads, down_grads)
            )
            from_mine = jnp.sum(spread.reshape(NZ, NY, 8, lanes).astype(F32), axis=1).astype(BF)
            from_mine = from_mine.transpose(1, 0, 2).reshape(8, half)
            from_other = swap_core(from_mine)
            break
        moved = lax.ppermute(grad_tile, "section", [(NS - 1 - step, NS - 2 - step)])
        grad_tile = jnp.where(section == NS - 2 - step, moved, up_tile)
        spread = exchange(jnp.broadcast_to(grad_tile[None], (NZ * NY, GROUP, lanes)))
        arrived = swap_core(spread)
        mine, other = unpack(spread), unpack(arrived)
        up_tile = grad_tile

    final = whole(from_mine, from_other)
    own_pair = jnp.where(core == 0, final[0:2], final[2:4])
    gain_grads = final[4].astype(F32) + final[5].astype(F32)
    return (
        own_pair[None, :, None],
        gate_grads[None],
        up_grads[None],
        down_grads[None],
        gain_grads[None],
    )


def solution(mesh):
    grid = Mesh(mesh.devices.reshape(NZ, NY, NC, NS), ("z", "y", "core", "section"))
    return jax.shard_map(
        on_device,
        mesh=grid,
        in_specs=(
            P("section", None, DP, None),
            P(None, DP, None),
            P("section", DP, None),
            P("section", DP, None),
            P("section", DP, None),
            P("section", None),
            P(),
        ),
        out_specs=(
            P("section", None, DP, None),
            P("section", DP, None),
            P("section", DP, None),
            P("section", DP, None),
            P("section", None),
        ),
        check_vma=False,
    )
```

```python
import jax
import jax.numpy as jnp
from jax import lax
from jax.sharding import Mesh
from jax.sharding import PartitionSpec as P

NZ, NY, NC, NS = 8, 4, 2, 4
DP = ("z", "y", "core")
PLANE = ("y", "z")
LIVE = 85
PACK = 12
GROUP = 48
USED = 43
PARTS = 2
BLOCKS = NZ * NY // PARTS
ROWS = PARTS * GROUP
BF = jnp.bfloat16
F32 = jnp.float32


def dot_nt(a, b):
    return lax.dot_general(a, b, (((1,), (1,)), ((), ())), preferred_element_type=F32)


def dot_nn(a, b):
    return lax.dot_general(a, b, (((1,), (0,)), ((), ())), preferred_element_type=F32)


def dot_tn(a, b):
    return lax.dot_general(a, b, (((0,), (0,)), ((), ())), preferred_element_type=F32)


def row_of(micro, slot):
    position = jnp.where(micro == 0, slot, LIVE - 1 - slot)
    return GROUP * (position // USED) + position % USED


def swap_core(x):
    return lax.ppermute(x, "core", [(0, 1), (1, 0)])


def exchange(x):
    return lax.all_to_all(x, PLANE, 0, 0, tiled=True)


def packed_slot(counts, index, residue):
    first = jnp.clip((counts[0] - residue + NY * NC - 1) // (NY * NC), 0, NZ)
    micro = (index >= first).astype(jnp.int32)
    at_z = index - first * micro
    slot = at_z * NY * NC + residue
    return micro, at_z, slot, slot < jnp.where(micro == 0, counts[0], counts[1])


def packing(counts, y, core):
    shape = (4, PACK, NZ, 8)
    kind_half, index, z, piece = (lax.broadcasted_iota(jnp.int32, shape, d) for d in range(4))
    micro, at_z, _, live = packed_slot(counts, index, y * NC + core)
    hit = live & (at_z == z) & (piece == (kind_half // 2) * 4 + micro * 2 + kind_half % 2)
    return hit.astype(BF).reshape(4 * PACK, NZ * 8)


def spread_rows(own, weights, pack):
    count, half = own.shape
    along_z = lax.all_to_all(jnp.broadcast_to(own[None], (NZ, count, half)), "z", 0, 0, tiled=True)
    along_z, weights = lax.optimization_barrier((along_z, weights))
    packed = dot_nn(pack, along_z.reshape(NZ * count, half)).astype(BF)
    shifted = [packed]
    for by in (2, 1, 3):
        shifted.append(lax.ppermute(packed, "y", [(i, (i + by) % NY) for i in range(NY)]))
    swapped = [swap_core(x) for x in shifted]
    return jnp.concatenate(shifted, axis=0), jnp.concatenate(swapped, axis=0), weights


def selection(counts, y, core, first_half):
    shape = (4, ROWS, NY, 4, PACK)
    out, row, shift, kind_half, index = (lax.broadcasted_iota(jnp.int32, shape, d) for d in range(5))
    by = jnp.where(shift == 1, 2, jnp.where(shift == 2, 1, shift))
    micro, _, slot, live = packed_slot(counts, index, ((y - by + NY) % NY) * NC + core)
    hit = live & (row_of(micro, slot) == row) & (kind_half == (out ^ first_half))
    return hit.astype(BF).reshape(4 * ROWS, NY * 4 * PACK)


def gather_rows(hidden, top, weights, counts, y, core):
    half = hidden.shape[-1] // 2
    own = jnp.concatenate([hidden, top], axis=0).reshape(8, half)
    pack, pick_own, pick_other, wanted = lax.optimization_barrier(
        (
            packing(counts, y, core),
            selection(counts, y, core, core),
            selection(counts, y, 1 - core, core),
            wanted_rows(counts, y // 2),
        )
    )
    mine, other, weights = spread_rows(own, weights, pack)
    rows = (dot_nn(pick_own, mine) + dot_nn(pick_other, other)).astype(BF).reshape(2, 2, ROWS, half)
    return (rows[0, 0], rows[0, 1]), (rows[1, 0], rows[1, 1]), wanted, weights


def wanted_rows(counts, part):
    shape = (NZ * NY * 8, GROUP)
    index, row = (lax.broadcasted_iota(jnp.int32, shape, d) for d in range(2))
    place, piece = index // 8, index % 8
    slot = (place % NZ) * NY * NC + (place // NZ) * NC + piece // 2
    micro = piece % 2
    limit = jnp.where(micro == 0, counts[0], counts[1])
    hit = (piece < 4) & (row_of(micro, slot) == part * GROUP + row) & (slot < limit)
    carry = (part == 0) & ((piece == 4) & (row == USED) | (piece == 5) & (row == USED + 1))
    return (hit | carry).astype(BF)


def on_device(hidden_in, grad_out, weight_gate, weight_up, weight_down, gain, counts):
    gate_mat, up_mat, down_mat = weight_gate[0], weight_up[0], weight_down[0]
    gain_row = gain[0]
    width = gate_mat.shape[1]
    half = width // 2
    lanes = half // BLOCKS
    z, y, core = lax.axis_index("z"), lax.axis_index("y"), lax.axis_index("core")
    section = lax.axis_index("section")
    part, block = y // 2, (y % 2) * NZ + z

    def halves(x):
        return (
            lax.dynamic_slice_in_dim(x, core * half, half, 1),
            lax.dynamic_slice_in_dim(x, (1 - core) * half, half, 1),
        )

    def whole(own, away):
        return jnp.concatenate(
            [jnp.where(core == 0, own, away), jnp.where(core == 0, away, own)], axis=1
        )

    def unpack(x):
        return x.reshape(PARTS, BLOCKS, GROUP, lanes).transpose(0, 2, 1, 3).reshape(ROWS, half)

    units = gate_mat.shape[0]
    padded = -(-units // 256) * 256

    def pad_units(x):
        return jnp.pad(x, ((0, padded - units), (0, 0)))

    hidden, (mine, other), wanted, (gate_mat, up_mat, down_mat) = gather_rows(
        hidden_in[0, :, 0], grad_out[:, 0], (gate_mat, up_mat, down_mat), counts, y, core
    )
    gate_own, gate_away = halves(gate_mat)
    up_own, up_away = halves(up_mat)
    both_own = jnp.concatenate([pad_units(gate_own), pad_units(up_own)], axis=0)
    both_away = jnp.concatenate([pad_units(gate_away), pad_units(up_away)], axis=0)
    down_own, down_away = (pad_units(x) for x in halves(down_mat))
    both_own, both_away, down_own, down_away = lax.optimization_barrier(
        (both_own, both_away, down_own, down_away)
    )

    values = [x.astype(F32) for x in hidden]
    squares = sum(jnp.sum(x * x, axis=-1, keepdims=True) for x in values)
    inv_rms = lax.rsqrt(squares / width + 1e-05)
    gain_halves = halves(gain_row[None])
    unit_own, unit_away = (x * inv_rms for x in values)
    normed_own = (unit_own * gain_halves[0]).astype(BF)
    normed_away = (unit_away * gain_halves[1]).astype(BF)
    pre = dot_nt(normed_own, both_own) + dot_nt(normed_away, both_away)
    gate_pre, up_pre = pre[:, :padded], pre[:, padded:]
    sig = jax.nn.sigmoid(gate_pre)
    up_factor = gate_pre * sig
    activation = (up_factor * up_pre).astype(BF)
    gate_factor = up_pre * sig * (1.0 + gate_pre * (1.0 - sig))

    def tile_of(x):
        rows = lax.dynamic_slice_in_dim(x, part * GROUP, GROUP, 0)
        return lax.dynamic_slice_in_dim(rows, block * lanes, lanes, 1)

    hidden_tile = tile_of(hidden[0]).astype(F32)
    up_tile = tile_of(mine)
    inv_tile = lax.dynamic_slice_in_dim(inv_rms, part * GROUP, GROUP, 0)
    gain_tile = lax.dynamic_slice_in_dim(gain_row, core * half + block * lanes, lanes, 0)
    in_group = lax.broadcasted_iota(jnp.int32, (PARTS, GROUP, 1), 1)
    tile_row = lax.broadcasted_iota(jnp.int32, (GROUP, 1), 0)

    for step in range(NS):
        last = step == NS - 1
        grad_act = dot_nt(mine, down_own) + dot_nt(other, down_away)
        grad_gate = (grad_act * gate_factor).astype(BF)
        grad_up = (grad_act * up_factor).astype(BF)
        grads = jnp.concatenate([grad_gate, grad_up], axis=1)
        inner = jnp.sum(grad_gate.astype(F32) * gate_pre + grad_up.astype(F32) * up_pre, axis=1)
        inner = jnp.tile(jnp.pad(inner, (0, lanes - ROWS)), BLOCKS)

        def partial_of(weights, unit_rows):
            partial = dot_nn(grads, weights)
            packed = jnp.where(in_group == USED, inner, partial.reshape(PARTS, GROUP, half))
            if last:
                packed = jnp.where(in_group == USED + 1, jnp.sum(partial * unit_rows, axis=0), packed)
            return packed.astype(BF)

        away = swap_core(partial_of(both_away, unit_away))
        kept = partial_of(both_own, unit_own)
        summed = (kept.astype(F32) + away.astype(F32)).astype(BF)
        pieces = summed.reshape(PARTS, GROUP, BLOCKS, lanes).transpose(0, 2, 1, 3).reshape(NZ * NY, GROUP, lanes)
        if last:
            pieces, grad_gate, grad_up, spread, arrived = lax.optimization_barrier(
                (pieces, grad_gate, grad_up, spread, arrived)
            )
            upstream = whole(unpack(spread), unpack(arrived))
        total = jnp.sum(exchange(pieces).astype(F32), axis=0)
        row_sum = lax.dynamic_slice_in_dim(total[USED], part * GROUP, GROUP, 0)[:, None]
        grad_tile = (
            up_tile.astype(F32)
            + inv_tile * (gain_tile * total)
            - hidden_tile * inv_tile * inv_tile * row_sum / width
        )
        grad_tile = jnp.where(tile_row < USED, grad_tile, 0.0).astype(BF)
        if last:
            gain_sum = total[USED + 1]
            high = gain_sum.astype(BF)
            low = (gain_sum - high.astype(F32)).astype(BF)
            grad_tile = jnp.where(tile_row == USED, high, grad_tile)
            grad_tile = jnp.where(tile_row == USED + 1, low, grad_tile)
            sent = dot_nn(wanted, grad_tile).astype(BF).reshape(NZ * NY, 8, lanes)
            spread = exchange(sent)
            normed = whole(normed_own, normed_away)
            gate_grads = dot_tn(grad_gate[:, :units], normed).astype(BF)
            up_grads = dot_tn(grad_up[:, :units], normed).astype(BF)
            down_grads = dot_tn(activation[:, :units], upstream).astype(BF)
            spread, gate_grads, up_grads, down_grads = lax.optimization_barrier(
                (spread, gate_grads, up_grads, down_grads)
            )
            from_mine = jnp.sum(spread.reshape(PARTS, BLOCKS, 8, lanes).astype(F32), axis=0).astype(BF)
            from_mine = from_mine.transpose(1, 0, 2).reshape(8, half)
            from_other = swap_core(from_mine)
            break
        moved = lax.ppermute(grad_tile, "section", [(NS - 1 - step, NS - 2 - step)])
        grad_tile = jnp.where(section == NS - 2 - step, moved, up_tile)
        spread = exchange(jnp.broadcast_to(grad_tile[None], (NZ * NY, GROUP, lanes)))
        arrived = swap_core(spread)
        mine, other = unpack(spread), unpack(arrived)
        up_tile = grad_tile

    final = whole(from_mine, from_other)
    own_pair = jnp.where(core == 0, final[0:2], final[2:4])
    gain_grads = final[4].astype(F32) + final[5].astype(F32)
    return (
        own_pair[None, :, None],
        gate_grads[None],
        up_grads[None],
        down_grads[None],
        gain_grads[None],
    )


def solution(mesh):
    grid = Mesh(mesh.devices.reshape(NZ, NY, NC, NS), ("z", "y", "core", "section"))
    return jax.shard_map(
        on_device,
        mesh=grid,
        in_specs=(
            P("section", None, DP, None),
            P(None, DP, None),
            P("section", DP, None),
            P("section", DP, None),
            P("section", DP, None),
            P("section", None),
            P(),
        ),
        out_specs=(
            P("section", None, DP, None),
            P("section", DP, None),
            P("section", DP, None),
            P("section", DP, None),
            P("section", None),
        ),
        check_vma=False,
    )
```

```python
import jax
import jax.numpy as jnp
from jax import lax
from jax.sharding import Mesh
from jax.sharding import PartitionSpec as P

NZ, NY, NC, NS = 8, 4, 2, 4
DP = ("z", "y", "core")
PLANE = ("z", "y")
LIVE = 85
PACK = 12
GROUP = 48
USED = 43
PARTS = 2
BLOCKS = NZ * NY // PARTS
ROWS = PARTS * GROUP
BF = jnp.bfloat16
F32 = jnp.float32


def dot_nt(a, b):
    return lax.dot_general(a, b, (((1,), (1,)), ((), ())), preferred_element_type=F32)


def dot_nn(a, b):
    return lax.dot_general(a, b, (((1,), (0,)), ((), ())), preferred_element_type=F32)


def dot_tn(a, b):
    return lax.dot_general(a, b, (((0,), (0,)), ((), ())), preferred_element_type=F32)


def row_of(micro, slot):
    position = jnp.where(micro == 0, slot, LIVE - 1 - slot)
    return GROUP * (position // USED) + position % USED


def swap_core(x):
    return lax.ppermute(x, "core", [(0, 1), (1, 0)])


def exchange(x):
    return lax.all_to_all(x, PLANE, 0, 0, tiled=True)


def packed_slot(counts, index, residue):
    first = jnp.clip((counts[0] - residue + NY * NC - 1) // (NY * NC), 0, NZ)
    micro = (index >= first).astype(jnp.int32)
    at_z = index - first * micro
    slot = at_z * NY * NC + residue
    return micro, at_z, slot, slot < jnp.where(micro == 0, counts[0], counts[1])


def packing(counts, y, core):
    shape = (4, PACK, NZ, 8)
    kind_half, index, z, piece = (lax.broadcasted_iota(jnp.int32, shape, d) for d in range(4))
    micro, at_z, _, live = packed_slot(counts, index, y * NC + core)
    hit = live & (at_z == z) & (piece == (kind_half // 2) * 4 + micro * 2 + kind_half % 2)
    return hit.astype(BF).reshape(4 * PACK, NZ * 8)


def spread_rows(own, weights, pack):
    count, half = own.shape
    along_z = lax.all_to_all(jnp.broadcast_to(own[None], (NZ, count, half)), "z", 0, 0, tiled=True)
    along_z, weights = lax.optimization_barrier((along_z, weights))
    packed = dot_nn(pack, along_z.reshape(NZ * count, half)).astype(BF)
    shifted = [packed]
    for by in (2, 1, 3):
        shifted.append(lax.ppermute(packed, "y", [(i, (i + by) % NY) for i in range(NY)]))
    swapped = [swap_core(x) for x in shifted]
    return jnp.concatenate(shifted, axis=0), jnp.concatenate(swapped, axis=0), weights


def selection(counts, y, core, first_half):
    shape = (4, ROWS, NY, 4, PACK)
    out, row, shift, kind_half, index = (lax.broadcasted_iota(jnp.int32, shape, d) for d in range(5))
    by = jnp.where(shift == 1, 2, jnp.where(shift == 2, 1, shift))
    micro, _, slot, live = packed_slot(counts, index, ((y - by + NY) % NY) * NC + core)
    hit = live & (row_of(micro, slot) == row) & (kind_half == (out ^ first_half))
    return hit.astype(BF).reshape(4 * ROWS, NY * 4 * PACK)


def gather_rows(hidden, top, weights, counts, y, core):
    half = hidden.shape[-1] // 2
    own = jnp.concatenate([hidden, top], axis=0).reshape(8, half)
    pack, pick_own, pick_other, wanted = lax.optimization_barrier(
        (
            packing(counts, y, core),
            selection(counts, y, core, core),
            selection(counts, y, 1 - core, core),
            wanted_rows(counts, lax.axis_index("z") // 4),
        )
    )
    mine, other, weights = spread_rows(own, weights, pack)
    rows = (dot_nn(pick_own, mine) + dot_nn(pick_other, other)).astype(BF).reshape(2, 2, ROWS, half)
    return (rows[0, 0], rows[0, 1]), (rows[1, 0], rows[1, 1]), wanted, weights


def wanted_rows(counts, part):
    shape = (NZ * NY * 8, GROUP)
    index, row = (lax.broadcasted_iota(jnp.int32, shape, d) for d in range(2))
    place, piece = index // 8, index % 8
    slot = place * NC + piece // 2
    micro = piece % 2
    limit = jnp.where(micro == 0, counts[0], counts[1])
    hit = (piece < 4) & (row_of(micro, slot) == part * GROUP + row) & (slot < limit)
    carry = (part == 0) & ((piece == 4) & (row == USED) | (piece == 5) & (row == USED + 1))
    return (hit | carry).astype(BF)


def on_device(hidden_in, grad_out, weight_gate, weight_up, weight_down, gain, counts):
    gate_mat, up_mat, down_mat = weight_gate[0], weight_up[0], weight_down[0]
    gain_row = gain[0]
    width = gate_mat.shape[1]
    half = width // 2
    lanes = half // BLOCKS
    z, y, core = lax.axis_index("z"), lax.axis_index("y"), lax.axis_index("core")
    section = lax.axis_index("section")
    part, block = z // 4, (z % 4) * NY + y

    def halves(x):
        return (
            lax.dynamic_slice_in_dim(x, core * half, half, 1),
            lax.dynamic_slice_in_dim(x, (1 - core) * half, half, 1),
        )

    def whole(own, away):
        return jnp.concatenate(
            [jnp.where(core == 0, own, away), jnp.where(core == 0, away, own)], axis=1
        )

    def unpack(x):
        return x.reshape(PARTS, BLOCKS, GROUP, lanes).transpose(0, 2, 1, 3).reshape(ROWS, half)

    units = gate_mat.shape[0]
    padded = -(-units // 256) * 256

    def pad_units(x):
        return jnp.pad(x, ((0, padded - units), (0, 0)))

    hidden, (mine, other), wanted, (gate_mat, up_mat, down_mat) = gather_rows(
        hidden_in[0, :, 0], grad_out[:, 0], (gate_mat, up_mat, down_mat), counts, y, core
    )
    gate_own, gate_away = halves(gate_mat)
    up_own, up_away = halves(up_mat)
    both_own = jnp.concatenate([pad_units(gate_own), pad_units(up_own)], axis=0)
    both_away = jnp.concatenate([pad_units(gate_away), pad_units(up_away)], axis=0)
    down_own, down_away = (pad_units(x) for x in halves(down_mat))
    both_own, both_away, down_own, down_away = lax.optimization_barrier(
        (both_own, both_away, down_own, down_away)
    )

    values = [x.astype(F32) for x in hidden]
    squares = sum(jnp.sum(x * x, axis=-1, keepdims=True) for x in values)
    inv_rms = lax.rsqrt(squares / width + 1e-05)
    gain_halves = halves(gain_row[None])
    unit_own, unit_away = (x * inv_rms for x in values)
    normed_own = (unit_own * gain_halves[0]).astype(BF)
    normed_away = (unit_away * gain_halves[1]).astype(BF)
    pre = dot_nt(normed_own, both_own) + dot_nt(normed_away, both_away)
    gate_pre, up_pre = pre[:, :padded], pre[:, padded:]
    sig = jax.nn.sigmoid(gate_pre)
    up_factor = gate_pre * sig
    activation = (up_factor * up_pre).astype(BF)
    gate_factor = up_pre * sig * (1.0 + gate_pre * (1.0 - sig))

    def tile_of(x):
        rows = lax.dynamic_slice_in_dim(x, part * GROUP, GROUP, 0)
        return lax.dynamic_slice_in_dim(rows, block * lanes, lanes, 1)

    hidden_tile = tile_of(hidden[0]).astype(F32)
    up_tile = tile_of(mine)
    inv_tile = lax.dynamic_slice_in_dim(inv_rms, part * GROUP, GROUP, 0)
    gain_tile = lax.dynamic_slice_in_dim(gain_row, core * half + block * lanes, lanes, 0)
    in_group = lax.broadcasted_iota(jnp.int32, (PARTS, GROUP, 1), 1)
    tile_row = lax.broadcasted_iota(jnp.int32, (GROUP, 1), 0)

    for step in range(NS):
        last = step == NS - 1
        grad_act = dot_nt(mine, down_own) + dot_nt(other, down_away)
        grad_gate = (grad_act * gate_factor).astype(BF)
        grad_up = (grad_act * up_factor).astype(BF)
        grads = jnp.concatenate([grad_gate, grad_up], axis=1)
        inner = jnp.sum(grad_gate.astype(F32) * gate_pre + grad_up.astype(F32) * up_pre, axis=1)
        inner = jnp.tile(jnp.pad(inner, (0, lanes - ROWS)), BLOCKS)

        def partial_of(weights, unit_rows):
            partial = dot_nn(grads, weights)
            packed = jnp.where(in_group == USED, inner, partial.reshape(PARTS, GROUP, half))
            if last:
                packed = jnp.where(in_group == USED + 1, jnp.sum(partial * unit_rows, axis=0), packed)
            return packed.astype(BF)

        away = swap_core(partial_of(both_away, unit_away))
        kept = partial_of(both_own, unit_own)
        summed = (kept.astype(F32) + away.astype(F32)).astype(BF)
        pieces = summed.reshape(PARTS, GROUP, BLOCKS, lanes).transpose(0, 2, 1, 3).reshape(NZ * NY, GROUP, lanes)
        if last:
            pieces, grad_gate, grad_up, spread, arrived = lax.optimization_barrier(
                (pieces, grad_gate, grad_up, spread, arrived)
            )
            upstream = whole(unpack(spread), unpack(arrived))
        total = jnp.sum(exchange(pieces).astype(F32), axis=0)
        row_sum = lax.dynamic_slice_in_dim(total[USED], part * GROUP, GROUP, 0)[:, None]
        grad_tile = (
            up_tile.astype(F32)
            + inv_tile * (gain_tile * total)
            - hidden_tile * inv_tile * inv_tile * row_sum / width
        )
        grad_tile = jnp.where(tile_row < USED, grad_tile, 0.0).astype(BF)
        if last:
            gain_sum = total[USED + 1]
            high = gain_sum.astype(BF)
            low = (gain_sum - high.astype(F32)).astype(BF)
            grad_tile = jnp.where(tile_row == USED, high, grad_tile)
            grad_tile = jnp.where(tile_row == USED + 1, low, grad_tile)
            sent = dot_nn(wanted, grad_tile).astype(BF).reshape(NZ * NY, 8, lanes)
            spread = exchange(sent)
            normed = whole(normed_own, normed_away)
            gate_grads = dot_tn(grad_gate[:, :units], normed).astype(BF)
            up_grads = dot_tn(grad_up[:, :units], normed).astype(BF)
            down_grads = dot_tn(activation[:, :units], upstream).astype(BF)
            spread, gate_grads, up_grads, down_grads = lax.optimization_barrier(
                (spread, gate_grads, up_grads, down_grads)
            )
            from_mine = jnp.sum(spread.reshape(PARTS, BLOCKS, 8, lanes).astype(F32), axis=0).astype(BF)
            from_mine = from_mine.transpose(1, 0, 2).reshape(8, half)
            from_other = swap_core(from_mine)
            break
        moved = lax.ppermute(grad_tile, "section", [(NS - 1 - step, NS - 2 - step)])
        grad_tile = jnp.where(section == NS - 2 - step, moved, up_tile)
        spread = exchange(jnp.broadcast_to(grad_tile[None], (NZ * NY, GROUP, lanes)))
        arrived = swap_core(spread)
        mine, other = unpack(spread), unpack(arrived)
        up_tile = grad_tile

    final = whole(from_mine, from_other)
    own_pair = jnp.where(core == 0, final[0:2], final[2:4])
    gain_grads = final[4].astype(F32) + final[5].astype(F32)
    return (
        own_pair[None, :, None],
        gate_grads[None],
        up_grads[None],
        down_grads[None],
        gain_grads[None],
    )


def solution(mesh):
    grid = Mesh(mesh.devices.reshape(NZ, NY, NC, NS), ("z", "y", "core", "section"))
    return jax.shard_map(
        on_device,
        mesh=grid,
        in_specs=(
            P("section", None, DP, None),
            P(None, DP, None),
            P("section", DP, None),
            P("section", DP, None),
            P("section", DP, None),
            P("section", None),
            P(),
        ),
        out_specs=(
            P("section", None, DP, None),
            P("section", DP, None),
            P("section", DP, None),
            P("section", DP, None),
            P("section", None),
        ),
        check_vma=False,
    )
```
